128 devices in a mesh: grp: 8 (over x, z_lo), wide: 16 (over y, z_hi, core).
Axes of the slice: x: 4, y: 4, z: 4 (z_hi: 2, z_lo: 2; z = z_hi * 2 + z_lo), core: 2. Of those that a mesh axis runs over, the one named last changes fastest.
Arguments:
- left_env: bfloat16 [64, 32, 128, 128], P('grp', 'wide'), may hold values from -0.5 to 0.5
- right_env: bfloat16 [128, 32, 128, 128], P('wide', 'grp'), may hold values from -0.09375 to 0.09375
- psi: bfloat16 [64, 128, 128, 128], P('grp', 'wide'), may hold values from -6 to 6
- left_shift: int32 [32], replicated, may hold values from -1 to 1
- right_shift: int32 [32], replicated, may hold values from -1 to 1
- active: int32 [64, 128, 32], P('grp', 'wide'), may hold values 0 or 1
Outputs:
- hpsi: float32 [64, 128, 128, 128], P('grp', 'wide')
The draws below stay inside these ranges and needn't reach their ends.
All inputs are finite; a program needn't handle non-finite values. No bound on the sum of `active` on one device may be relied on, other than what follows from the above.
Results may differ from the reference program's by a relative error of at most 0.0029.
Values may be sent and summed in bfloat16 or wider, within the bound.
No kernel may reach another device: no remote copies, remote signals or barrier semaphores. Data moves between devices by JAX's collectives and lax.ppermute only.
A program may use at most 128 MiB of HBM per device.

```python
import jax
import jax.numpy as jnp
from jax import lax

B = 128
W = 32
SL = 64
SR = 128


def touch_ends(entries, key, low, largest):
    longest = entries.shape.index(max(entries.shape))
    spots = []
    for shift in (0, 1):
        where = [jax.random.randint(jax.random.fold_in(key, axis), (), 0, length) for axis, length in enumerate(entries.shape)]
        where[longest] = (where[longest] + shift) % entries.shape[longest]
        spots.append(tuple(where))
    return entries.at[spots[0]].set(low).at[spots[1]].set(largest)


def levels(rng, extent, pieces, low, top_value):
    loudness = 1.0
    for dim, shards_of in pieces:
        draws = jax.random.uniform(jax.random.fold_in(jax.random.fold_in(rng, 6), dim), (shards_of,), jnp.float32, low / len(pieces), top_value / len(pieces))
        loudness = loudness * jnp.repeat(jnp.exp(draws), extent[dim] // shards_of).reshape((-1,) + (1,) * (len(extent) - 1 - dim))
    return loudness


def noise(own_key, extent, width, limit, shards=(), kind=jnp.bfloat16):
    values = width * jax.random.normal(own_key, extent, jnp.float32)
    if shards:
        values = values * levels(own_key, extent, shards, -0.22, 0.18)
    return jnp.clip(values, -limit, limit).astype(kind)


def setup_inputs(seed: int = 0) -> dict:
    splits = jax.random.split(jax.random.key(seed), 7)
    left_env = noise(splits[0], (SL, W, B, B), B ** -0.5, 0.5, ((0, 8), (1, 16)))
    right_env = noise(splits[1], (SR, W, B, B), (B * W) ** -0.5, 0.09375, ((0, 16), (1, 8)))
    psi = noise(splits[2], (SL, SR, B, B), 1.0, 6.0, ((0, 8), (1, 16)))
    left_shift = touch_ends(jax.random.randint(splits[3], (W,), -1, 2), jax.random.fold_in(splits[3], 1), -1, 1).astype(jnp.int32)
    right_shift = touch_ends(jax.random.randint(splits[4], (W,), -1, 2), jax.random.fold_in(splits[4], 1), -1, 1).astype(jnp.int32)
    active = touch_ends((jax.random.randint(splits[5], (SL, SR, W), 0, 4) < 3).astype(jnp.int32), jax.random.fold_in(splits[5], 1), 0, 1)
    return dict(left_env=left_env, right_env=right_env, psi=psi, left_shift=left_shift, right_shift=right_shift, active=active)


def reference(left_env, right_env, psi, left_shift, right_shift, active):
    padded = jnp.pad(psi, ((1, 1), (1, 1), (0, 0), (0, 0)))
    right_full = right_env.astype(jnp.float32)
    col_ids = jnp.arange(SR, dtype=jnp.int32)[None, :] + 1 + right_shift.astype(jnp.int32)[:, None]

    def one_row(row_index):
        row_ids = row_index + 1 + left_shift.astype(jnp.int32)
        picked = padded[row_ids[:, None], col_ids].astype(jnp.float32)
        left_row = left_env[row_index].astype(jnp.float32)
        inner = jnp.einsum('wij,wcjk->wcik', left_row, picked).astype(jnp.bfloat16)
        inner = lax.optimization_barrier(inner).astype(jnp.float32)
        enabled = jnp.transpose(active[row_index]).astype(jnp.float32)
        inner = inner * enabled[:, :, None, None]
        return jnp.einsum('wcik,cwdk->cid', inner, right_full)

    return lax.map(one_row, jnp.arange(SL, dtype=jnp.int32))
```

```python
import functools

import jax
import jax.numpy as jnp
from jax import lax
from jax.experimental import pallas as pl
from jax.experimental.pallas import tpu as pltpu
from jax.sharding import Mesh, PartitionSpec as P

GRP = ("x", "zl")
WIDE = ("y", "zh", "core")
SIZES = (4, 2, 4, 2, 2)
B = 128
ROWS = 8
COLS = 8
TERMS = 4


def terms_kernel(layout, offsets, first, place, ls, rs, act, *refs):
    la, lac, lz, lzc, psi, up, down, west, east = refs[:9]
    rights, rest = [], refs[9:]
    for pieces in layout:
        rights.append(rest[:pieces])
        rest = rest[pieces:]
    if first:
        hout, lbuf, rbuf, grid, inner, psem, lsem, rsem = rest
    else:
        hin, hout, lbuf, rbuf, grid, inner, psem, lsem, rsem = rest
    steps = len(layout)
    n = pl.program_id(0)
    here = place[0]
    core, zh, y, zl, x = here & 1, (here >> 1) & 1, (here >> 2) & 3, (here >> 4) & 1, here >> 5

    def chunk(step):
        return (x + offsets[step][0]) & 3, (zl + offsets[step][1]) & 1

    def left_copies(step, slot, own):
        p, _ = chunk(step)
        a, b, where = (la, lac, p) if own else (lz, lzc, (p - y) & 3)
        return (
            pltpu.make_async_copy(a.at[where], lbuf.at[slot, core], lsem.at[slot, 0]),
            pltpu.make_async_copy(b.at[where], lbuf.at[slot, 1 - core], lsem.at[slot, 1]),
        )

    def right_copies(step, slot):
        pieces = rights[step]
        sources = pieces if len(pieces) == 2 else [pieces[0].at[pl.ds(4 * h, 4)] for h in range(2)]
        return [
            pltpu.make_async_copy(sources[h], rbuf.at[slot, pl.ds(4 * h, 4)], rsem.at[slot, h])
            for h in range(2)
        ]

    def fetch(step, slot):
        for copy in right_copies(step, slot):
            copy.start()

        @pl.when(chunk(step)[1] == zh)
        def _():
            for copy in left_copies(step, slot, True):
                copy.start()

        @pl.when(chunk(step)[1] != zh)
        def _():
            for copy in left_copies(step, slot, False):
                copy.start()

    psi_copies = [
        pltpu.make_async_copy(psi, grid.at[pl.ds(1, ROWS), pl.ds(1, COLS)], psem.at[0]),
        pltpu.make_async_copy(up, grid.at[pl.ds(0, 1), pl.ds(1, COLS)], psem.at[1]),
        pltpu.make_async_copy(down, grid.at[pl.ds(ROWS + 1, 1), pl.ds(1, COLS)], psem.at[2]),
        pltpu.make_async_copy(west, grid.at[:, pl.ds(0, 1)], psem.at[3]),
        pltpu.make_async_copy(east, grid.at[:, pl.ds(COLS + 1, 1)], psem.at[4]),
    ]

    @pl.when(n == 0)
    def _():
        for copy in psi_copies:
            copy.start()
        fetch(0, 0)

    for step in range(1, steps):

        @pl.when(n == step - 1)
        def _():
            fetch(step, step % 2)

    @pl.when(n == 0)
    def _():
        for copy in psi_copies:
            copy.wait()

    slot = lax.rem(n, 2)
    for copy in left_copies(0, slot, True):
        copy.wait()
    for copy in right_copies(0, slot):
        copy.wait()

    base = 0
    for step in range(steps):
        p, q = chunk(step)
        base = jnp.where(n == step, TERMS * (2 * p + q), base)

    def one_row(row, carry):
        for w in range(TERMS):
            picked = grid[row + 1 + ls[base + w], pl.ds(1 + rs[base + w], COLS)]
            joined = jnp.concatenate([picked[c] for c in range(COLS)], axis=1)
            part = jnp.dot(lbuf[slot, w // 2, row, w % 2], joined, preferred_element_type=jnp.float32)
            for c in range(COLS):
                on = act[row, c, base + w].astype(jnp.float32)
                inner[c, pl.ds(pl.multiple_of(row * B, B), B), w * B : (w + 1) * B] = (
                    part[:, c * B : (c + 1) * B] * on
                ).astype(jnp.bfloat16)
        return carry

    lax.fori_loop(0, ROWS, one_row, 0, unroll=True)

    for c in range(COLS):
        joined = jnp.concatenate([rbuf[slot, c, w] for w in range(TERMS)], axis=1)
        part = lax.dot_general(
            inner[c], joined, (((1,), (1,)), ((), ())), preferred_element_type=jnp.float32
        ).reshape(ROWS, B, B)

        @pl.when(n == 0)
        def _():
            hout[:, c] = part if first else hin[:, c] + part

        @pl.when(n != 0)
        def _():
            hout[:, c] += part


def add_terms(offsets, place, ls, rs, act, lefts, psis, rights, total):
    steps = len(rights)
    layout = tuple(len(pieces) for pieces in rights)
    first = total is None
    anywhere = pl.BlockSpec(memory_space=pl.ANY)
    whole = pl.BlockSpec((ROWS, COLS, B, B), lambda n, *_: (0, 0, 0, 0), pipeline_mode=pl.Buffered(1))
    operands = [*lefts, *psis, *(piece for pieces in rights for piece in pieces)]
    in_specs = [anywhere] * len(operands)
    if not first:
        operands.append(total)
        in_specs.append(whole)
    return pl.pallas_call(
        functools.partial(terms_kernel, layout, offsets, first),
        out_shape=jax.ShapeDtypeStruct((ROWS, COLS, B, B), jnp.float32),
        grid_spec=pltpu.PrefetchScalarGridSpec(
            num_scalar_prefetch=4,
            grid=(steps,),
            in_specs=in_specs,
            out_specs=whole,
            scratch_shapes=[
                pltpu.VMEM((2, 2, ROWS, 2, B, B), jnp.bfloat16),
                pltpu.VMEM((2, COLS, TERMS, B, B), jnp.bfloat16),
                pltpu.VMEM((ROWS + 2, COLS + 2, B, B), jnp.bfloat16),
                pltpu.VMEM((COLS, ROWS * B, TERMS * B), jnp.bfloat16),
                pltpu.SemaphoreType.DMA((5,)),
                pltpu.SemaphoreType.DMA((2, 2)),
                pltpu.SemaphoreType.DMA((2, 2)),
            ],
        ),
        input_output_aliases={} if first else {4 + len(operands) - 1: 0},
        compiler_params=pltpu.CompilerParams(
            vmem_limit_bytes=56 << 20, dimension_semantics=("arbitrary",)
        ),
        cost_estimate=pl.CostEstimate(
            flops=steps * 2 * 2 * ROWS * COLS * TERMS * B**3,
            bytes_accessed=(steps * 2 + 11) << 20,
            transcendentals=0,
        ),
    )(place, ls, rs, act, *operands)


def ring(value, axis, shift):
    return lax.ppermute(value, axis, [(i, (i + shift) % 4) for i in range(4)])


def swap(value, axis):
    return lax.ppermute(value, axis, [(0, 1), (1, 0)])


def edges(value, axes, dim):
    count = lax.axis_size(axes)
    length = value.shape[dim]
    up = [(i, i + 1) for i in range(count - 1)]
    down = [(j, i) for i, j in up]
    last = lax.slice_in_dim(value, length - 1, length, axis=dim)
    leading = lax.slice_in_dim(value, 0, 1, axis=dim)
    return lax.ppermute(last, axes, up), lax.ppermute(leading, axes, down)


def after(values, events):
    held = lax.optimization_barrier((tuple(values), tuple(events)))
    return held[0]


def per_device(left_env, right_env, psi, left_shift, right_shift, active):
    place = lax.axis_index((*GRP, *WIDE)).astype(jnp.int32)[None]

    left_y = lax.all_gather(left_env, "y", axis=0)
    right_m = ring(right_env, "x", 1)
    right_p = ring(right_env, "x", -1)
    left_z = swap(left_env, "zh")
    north, south = edges(psi, GRP, 0)

    right_m, right_p, left_z, north, south, own = after(
        (right_m, right_p, left_z, north, south, right_env), ()
    )
    right_z = swap(own, "zl")
    far_0 = ring(right_m[:4], "x", 1)
    far_1 = ring(right_p[4:], "x", -1)
    left_zm = ring(left_z, "y", 1)
    left_zp = ring(left_z, "y", -1)
    left_z2 = ring(left_z, "y", 2)
    sides = jnp.concatenate([north[:, ::7], psi[:, ::7], south[:, ::7]], axis=0)
    west = lax.ppermute(sides[:, 1:], WIDE, [(i, i + 1) for i in range(15)])
    east = lax.ppermute(sides[:, :1], WIDE, [(i + 1, i) for i in range(15)])

    right_z, far_0, far_1 = after((right_z, far_0, far_1), ())
    right_zm = ring(right_z, "x", 1)
    right_zp = ring(right_z, "x", -1)
    far_z0 = swap(far_0, "zl")
    far_z1 = swap(far_1, "zl")
    left_yc = swap(left_y, "core")
    left_zs = jnp.stack([left_z, left_zp, left_z2, left_zm])
    left_zc = swap(left_zs, "core")

    shared = (
        place,
        left_shift,
        right_shift,
        active,
        (left_y, left_yc, left_zs, left_zc),
        (psi, north, south, west, east),
    )
    total = add_terms(
        ((0, 0), (0, 1), (3, 0), (1, 0), (2, 0)),
        *shared,
        [(right_env,), (right_z,), (right_m,), (right_p,), (far_0, far_1)],
        None,
    )
    return add_terms(
        ((3, 1), (1, 1), (2, 1)),
        *shared,
        [(right_zm,), (right_zp,), (far_z0, far_z1)],
        total,
    )


def solution(mesh):
    fine = Mesh(mesh.devices.reshape(SIZES), (*GRP, *WIDE))
    return jax.shard_map(
        per_device,
        mesh=fine,
        in_specs=(
            P(GRP, WIDE, None, None),
            P(WIDE, GRP, None, None),
            P(GRP, WIDE, None, None),
            P(),
            P(),
            P(GRP, WIDE, None),
        ),
        out_specs=P(GRP, WIDE, None, None),
        check_vma=False,
    )
```

```python
import functools

import jax
import jax.numpy as jnp
from jax import lax
from jax.experimental import pallas as pl
from jax.experimental.pallas import tpu as pltpu
from jax.sharding import Mesh, PartitionSpec as P

GRP = ("x", "zl")
WIDE = ("y", "zh", "core")
SIZES = (4, 2, 4, 2, 2)
B = 128
ROWS = 8
COLS = 8
TERMS = 4


def terms_kernel(layout, offsets, whole_ring, first, place, ls, rs, act, *refs):
    left, left_other, psi, up, down, west, east = refs[:7]
    rights, rest = [], refs[7:]
    for pieces in layout:
        rights.append(rest[:pieces])
        rest = rest[pieces:]
    if first:
        hout, lbuf, rbuf, grid, inner, psem, lsem, rsem = rest
    else:
        hin, hout, lbuf, rbuf, grid, inner, psem, lsem, rsem = rest
    steps = len(layout)
    n = pl.program_id(0)
    here = place[0]
    core, zh, y, zl, x = here & 1, (here >> 1) & 1, (here >> 2) & 3, (here >> 4) & 1, here >> 5

    def chunk(step):
        return (x + offsets[step][0]) & 3, (zl + offsets[step][1]) & 1

    def left_copies(step, slot):
        p, _ = chunk(step)
        where = p if whole_ring else (p - y) & 3
        return (
            pltpu.make_async_copy(left.at[where], lbuf.at[slot, core], lsem.at[slot, 0]),
            pltpu.make_async_copy(left_other.at[where], lbuf.at[slot, 1 - core], lsem.at[slot, 1]),
        )

    def right_copies(step, slot):
        pieces = rights[step]
        sources = pieces if len(pieces) == 2 else [pieces[0].at[pl.ds(4 * h, 4)] for h in range(2)]
        return [
            pltpu.make_async_copy(sources[h], rbuf.at[slot, pl.ds(4 * h, 4)], rsem.at[slot, h])
            for h in range(2)
        ]

    def fetch(step, slot):
        for copy in (*left_copies(step, slot), *right_copies(step, slot)):
            copy.start()

    psi_copies = [
        pltpu.make_async_copy(psi, grid.at[pl.ds(1, ROWS), pl.ds(1, COLS)], psem.at[0]),
        pltpu.make_async_copy(up, grid.at[pl.ds(0, 1), pl.ds(1, COLS)], psem.at[1]),
        pltpu.make_async_copy(down, grid.at[pl.ds(ROWS + 1, 1), pl.ds(1, COLS)], psem.at[2]),
        pltpu.make_async_copy(west, grid.at[:, pl.ds(0, 1)], psem.at[3]),
        pltpu.make_async_copy(east, grid.at[:, pl.ds(COLS + 1, 1)], psem.at[4]),
    ]

    @pl.when(n == 0)
    def _():
        for copy in psi_copies:
            copy.start()
        fetch(0, 0)

    for step in range(1, steps):

        @pl.when(n == step - 1)
        def _():
            fetch(step, step % 2)

    @pl.when(n == 0)
    def _():
        hout[...] = jnp.zeros_like(hout) if first else hin[...]
        for copy in psi_copies:
            copy.wait()

    slot = lax.rem(n, 2)
    for copy in left_copies(0, slot):
        copy.wait()
    for copy in right_copies(0, slot):
        copy.wait()

    base = 0
    for step in range(steps):
        p, q = chunk(step)
        base = jnp.where(n == step, TERMS * (2 * p + q), base)

    def one_row(row, carry):
        for w in range(TERMS):
            picked = grid[row + 1 + ls[base + w], pl.ds(1 + rs[base + w], COLS)]
            joined = jnp.concatenate([picked[c] for c in range(COLS)], axis=1)
            part = jnp.dot(lbuf[slot, w // 2, row, w % 2], joined, preferred_element_type=jnp.float32)
            for c in range(COLS):
                on = act[row, c, base + w].astype(jnp.float32)
                inner[c, pl.ds(pl.multiple_of(row * B, B), B), w * B : (w + 1) * B] = (
                    part[:, c * B : (c + 1) * B] * on
                ).astype(jnp.bfloat16)
        return carry

    lax.fori_loop(0, ROWS, one_row, 0, unroll=True)

    for c in range(COLS):
        joined = jnp.concatenate([rbuf[slot, c, w] for w in range(TERMS)], axis=1)
        part = lax.dot_general(
            inner[c], joined, (((1,), (1,)), ((), ())), preferred_element_type=jnp.float32
        ).reshape(ROWS, B, B)

        hout[:, c] += part


def add_terms(offsets, whole_ring, lefts, place, ls, rs, act, psis, rights, total):
    steps = len(rights)
    layout = tuple(len(pieces) for pieces in rights)
    first = total is None
    anywhere = pl.BlockSpec(memory_space=pl.ANY)
    whole = pl.BlockSpec((ROWS, COLS, B, B), lambda n, *_: (0, 0, 0, 0), pipeline_mode=pl.Buffered(1))
    operands = [*lefts, *psis, *(piece for pieces in rights for piece in pieces)]
    in_specs = [anywhere] * len(operands)
    if not first:
        operands.append(total)
        in_specs.append(whole)
    return pl.pallas_call(
        functools.partial(terms_kernel, layout, offsets, whole_ring, first),
        out_shape=jax.ShapeDtypeStruct((ROWS, COLS, B, B), jnp.float32),
        grid_spec=pltpu.PrefetchScalarGridSpec(
            num_scalar_prefetch=4,
            grid=(steps,),
            in_specs=in_specs,
            out_specs=whole,
            scratch_shapes=[
                pltpu.VMEM((2, 2, ROWS, 2, B, B), jnp.bfloat16),
                pltpu.VMEM((2, COLS, TERMS, B, B), jnp.bfloat16),
                pltpu.VMEM((ROWS + 2, COLS + 2, B, B), jnp.bfloat16),
                pltpu.VMEM((COLS, ROWS * B, TERMS * B), jnp.bfloat16),
                pltpu.SemaphoreType.DMA((5,)),
                pltpu.SemaphoreType.DMA((2, 2)),
                pltpu.SemaphoreType.DMA((2, 2)),
            ],
        ),
        input_output_aliases={} if first else {4 + len(operands) - 1: 0},
        compiler_params=pltpu.CompilerParams(
            vmem_limit_bytes=56 << 20, dimension_semantics=("arbitrary",)
        ),
        cost_estimate=pl.CostEstimate(flops=1, bytes_accessed=1, transcendentals=0),
    )(place, ls, rs, act, *operands)


def ring(value, axis, shift):
    return lax.ppermute(value, axis, [(i, (i + shift) % 4) for i in range(4)])


def swap(value, axis):
    return lax.ppermute(value, axis, [(0, 1), (1, 0)])


def edges(value, axes, dim):
    count = lax.axis_size(axes)
    length = value.shape[dim]
    up = [(i, i + 1) for i in range(count - 1)]
    down = [(j, i) for i, j in up]
    last = lax.slice_in_dim(value, length - 1, length, axis=dim)
    leading = lax.slice_in_dim(value, 0, 1, axis=dim)
    return lax.ppermute(last, axes, up), lax.ppermute(leading, axes, down)


def after(values, events):
    held = lax.optimization_barrier((tuple(values), tuple(events)))
    return held[0]


def per_device(left_env, right_env, psi, left_shift, right_shift, active):
    place = lax.axis_index((*GRP, *WIDE)).astype(jnp.int32)[None]
    matched = lax.axis_index("zl") == lax.axis_index("zh")

    low, high = right_env[:4], right_env[4:]
    low_m = ring(low, "x", 1)
    high_p = ring(high, "x", -1)
    left_z = swap(left_env, "zh")
    north, south = edges(psi, GRP, 0)

    left_z, north, south, low_m, high_p, low, high, own = after(
        (left_z, north, south, low_m, high_p, low, high, right_env), ()
    )
    near = jnp.where(matched, left_env, left_z)
    other = jnp.where(matched, left_z, left_env)
    other_y = lax.all_gather(other, "y", axis=0)
    right_z = swap(own, "zl")
    near_m = ring(near, "y", 1)
    near_p = ring(near, "y", -1)
    high_m = ring(high, "x", 1)
    low_p = ring(low, "x", -1)

    far_0 = ring(low_m, "x", 1)
    far_1 = ring(high_p, "x", -1)
    near_2 = ring(near, "y", 2)
    sides = jnp.concatenate([north[:, ::7], psi[:, ::7], south[:, ::7]], axis=0)
    west = lax.ppermute(sides[:, 1:], WIDE, [(i, i + 1) for i in range(15)])
    east = lax.ppermute(sides[:, :1], WIDE, [(i + 1, i) for i in range(15)])

    right_z, far_0, far_1, high_m, low_p, near_2, west, east = after(
        (right_z, far_0, far_1, high_m, low_p, near_2, west, east), ()
    )
    right_zm = ring(right_z, "x", 1)
    right_zp = ring(right_z, "x", -1)
    far_z0 = swap(far_0, "zl")
    far_z1 = swap(far_1, "zl")
    near_y = jnp.stack([near, near_p, near_2, near_m])
    near_yc = swap(near_y, "core")

    shared = (place, left_shift, right_shift, active, (psi, north, south, west, east))
    nears = (near_y, near_yc)
    other_yc = swap(other_y, "core")
    total = add_terms(
        ((0, 0), (3, 0), (1, 0), (2, 0)),
        False,
        nears,
        *shared,
        [(right_env,), (low_m, high_m), (low_p, high_p), (far_0, far_1)],
        None,
    )
    return add_terms(
        ((0, 1), (3, 1), (1, 1), (2, 1)),
        True,
        (other_y, other_yc),
        *shared,
        [(right_z,), (right_zm,), (right_zp,), (far_z0, far_z1)],
        total,
    )


def solution(mesh):
    fine = Mesh(mesh.devices.reshape(SIZES), (*GRP, *WIDE))
    return jax.shard_map(
        per_device,
        mesh=fine,
        in_specs=(
            P(GRP, WIDE, None, None),
            P(WIDE, GRP, None, None),
            P(GRP, WIDE, None, None),
            P(),
            P(),
            P(GRP, WIDE, None),
        ),
        out_specs=P(GRP, WIDE, None, None),
        check_vma=False,
    )
```

```python
import functools

import jax
import jax.numpy as jnp
from jax import lax
from jax.experimental import pallas as pl
from jax.experimental.pallas import tpu as pltpu
from jax.sharding import Mesh, PartitionSpec as P

GRP = ("x", "zl")
WIDE = ("y", "zh", "core")
SIZES = (4, 2, 4, 2, 2)
B = 128
ROWS = 8
COLS = 8
TERMS = 4


def terms_kernel(span, layout, offsets, mode, place, ls, rs, act, *refs):
    start, rows = span
    left, psi, north, south, west, east = refs[:6]
    rights, rest = [], refs[6:]
    for pieces in layout:
        rights.append(rest[:pieces])
        rest = rest[pieces:]
    hin = None
    if mode != "new":
        hin, rest = rest[0], rest[1:]
    hout, lbuf, rbuf, grid, inner, psem, lsem, rsem = rest
    steps = len(layout)
    n = pl.program_id(0)
    here = place[0]
    zl, x = (here >> 4) & 1, here >> 5

    def first_term(step):
        return TERMS * (2 * ((x + offsets[step][0]) & 3) + ((zl + offsets[step][1]) & 1))

    def copies(step, slot):
        pieces = rights[step]
        sources = pieces if len(pieces) == 2 else [pieces[0].at[pl.ds(4 * h, 4)] for h in range(2)]
        return [
            pltpu.make_async_copy(left.at[:, pl.ds(first_term(step), TERMS)], lbuf.at[slot], lsem.at[slot]),
            *(
                pltpu.make_async_copy(sources[h], rbuf.at[slot, pl.ds(4 * h, 4)], rsem.at[slot, h])
                for h in range(2)
            ),
        ]

    low, high = max(start - 1, 0), min(start + rows + 1, ROWS)
    psi_copies = [
        pltpu.make_async_copy(
            psi.at[pl.ds(low, high - low)],
            grid.at[pl.ds(low - start + 1, high - low), pl.ds(1, COLS)],
            psem.at[0],
        ),
        pltpu.make_async_copy(west.at[pl.ds(start, rows + 2)], grid.at[:, pl.ds(0, 1)], psem.at[1]),
        pltpu.make_async_copy(east.at[pl.ds(start, rows + 2)], grid.at[:, pl.ds(COLS + 1, 1)], psem.at[2]),
    ]
    if start == 0:
        psi_copies.append(pltpu.make_async_copy(north, grid.at[pl.ds(0, 1), pl.ds(1, COLS)], psem.at[3]))
    if start + rows == ROWS:
        psi_copies.append(
            pltpu.make_async_copy(south, grid.at[pl.ds(rows + 1, 1), pl.ds(1, COLS)], psem.at[4])
        )

    @pl.when(n == 0)
    def _():
        for copy in (*psi_copies, *copies(0, 0)):
            copy.start()

    for step in range(1, steps):

        @pl.when(n == step - 1)
        def _():
            for copy in copies(step, step % 2):
                copy.start()

    @pl.when(n == 0)
    def _():
        hout[...] = hin[...] if mode == "add" else jnp.zeros_like(hout)
        for copy in psi_copies:
            copy.wait()

    slot = lax.rem(n, 2)
    for copy in copies(0, slot):
        copy.wait()

    base = 0
    for step in range(steps):
        base = jnp.where(n == step, first_term(step), base)

    def one_row(row, carry):
        for w in range(TERMS):
            picked = grid[row + 1 + ls[base + w], pl.ds(1 + rs[base + w], COLS)]
            joined = jnp.concatenate([picked[c] for c in range(COLS)], axis=1)
            part = jnp.dot(lbuf[slot, row, w], joined, preferred_element_type=jnp.float32)
            for c in range(COLS):
                on = act[start + row, c, base + w].astype(jnp.float32)
                inner[c, pl.ds(pl.multiple_of(row * B, B), B), w * B : (w + 1) * B] = (
                    part[:, c * B : (c + 1) * B] * on
                ).astype(jnp.bfloat16)
        return carry

    lax.fori_loop(0, rows, one_row, 0, unroll=True)

    for c in range(COLS):
        joined = jnp.concatenate([rbuf[slot, c, w] for w in range(TERMS)], axis=1)
        part = lax.dot_general(
            inner[c], joined, (((1,), (1,)), ((), ())), preferred_element_type=jnp.float32
        ).reshape(rows, B, B)
        hout[:, c] += part


def add_terms(span, offsets, left, place, ls, rs, act, psis, rights, total, mode):
    start, rows = span
    steps = len(rights)
    layout = tuple(len(pieces) for pieces in rights)
    anywhere = pl.BlockSpec(memory_space=pl.ANY)
    block = pl.BlockSpec(
        (rows, COLS, B, B), lambda n, *_: (start // rows, 0, 0, 0), pipeline_mode=pl.Buffered(1)
    )
    operands = [left, *psis, *(piece for pieces in rights for piece in pieces)]
    in_specs = [anywhere] * len(operands)
    if mode != "new":
        operands.append(total)
        in_specs.append(block if mode == "add" else anywhere)
    return pl.pallas_call(
        functools.partial(terms_kernel, span, layout, offsets, mode),
        out_shape=jax.ShapeDtypeStruct((ROWS, COLS, B, B), jnp.float32),
        grid_spec=pltpu.PrefetchScalarGridSpec(
            num_scalar_prefetch=4,
            grid=(steps,),
            in_specs=in_specs,
            out_specs=block,
            scratch_shapes=[
                pltpu.VMEM((2, rows, TERMS, B, B), jnp.bfloat16),
                pltpu.VMEM((2, COLS, TERMS, B, B), jnp.bfloat16),
                pltpu.VMEM((rows + 2, COLS + 2, B, B), jnp.bfloat16),
                pltpu.VMEM((COLS, rows * B, TERMS * B), jnp.bfloat16),
                pltpu.SemaphoreType.DMA((5,)),
                pltpu.SemaphoreType.DMA((2,)),
                pltpu.SemaphoreType.DMA((2, 2)),
            ],
        ),
        input_output_aliases={} if mode == "new" else {4 + len(operands) - 1: 0},
        compiler_params=pltpu.CompilerParams(
            vmem_limit_bytes=56 << 20, dimension_semantics=("arbitrary",)
        ),
        cost_estimate=pl.CostEstimate(
            flops=steps * 4 * rows * COLS * TERMS * B**3,
            bytes_accessed=steps << 21,
            transcendentals=0,
        ),
    )(place, ls, rs, act, *operands)


def ring(value, axis, shift):
    return lax.ppermute(value, axis, [(i, (i + shift) % 4) for i in range(4)])


def swap(value, axis):
    return lax.ppermute(value, axis, [(0, 1), (1, 0)])


def edges(value, axes, dim):
    count = lax.axis_size(axes)
    length = value.shape[dim]
    up = [(i, i + 1) for i in range(count - 1)]
    down = [(j, i) for i, j in up]
    last = lax.slice_in_dim(value, length - 1, length, axis=dim)
    leading = lax.slice_in_dim(value, 0, 1, axis=dim)
    return lax.ppermute(last, axes, up), lax.ppermute(leading, axes, down)


def after(values, events):
    held = lax.optimization_barrier((tuple(values), tuple(events)))
    return held[0]


def per_device(left_env, right_env, psi, left_shift, right_shift, active):
    place = lax.axis_index((*GRP, *WIDE)).astype(jnp.int32)[None]

    spans = ((0, 4), (4, 2), (6, 2))
    lefts = [
        lax.all_gather(left_env[start : start + rows], WIDE, axis=1, tiled=True) for start, rows in spans
    ]

    right_m = ring(right_env, "x", 1)
    right_p = ring(right_env, "x", -1)
    right_z = swap(right_env, "zl")
    north, south = edges(psi, GRP, 0)

    right_m, right_p, right_z, north, south = after((right_m, right_p, right_z, north, south), ())
    far_0 = ring(right_m[:4], "x", 1)
    far_1 = ring(right_p[4:], "x", -1)
    right_zm = ring(right_z, "x", 1)
    right_zp = ring(right_z, "x", -1)
    sides = jnp.concatenate([north[:, ::7], psi[:, ::7], south[:, ::7]], axis=0)
    west = lax.ppermute(sides[:, 1:], WIDE, [(i, i + 1) for i in range(15)])
    east = lax.ppermute(sides[:, :1], WIDE, [(i + 1, i) for i in range(15)])
    far_z0 = swap(far_0, "zl")
    far_z1 = swap(far_1, "zl")

    shared = (place, left_shift, right_shift, active, (psi, north, south, west, east))
    early = [(right_env,), (right_z,), (right_m,), (right_p,), (far_0, far_1)]
    late = [(right_zm,), (right_zp,), (far_z0, far_z1)]
    early_at = ((0, 0), (0, 1), (3, 0), (1, 0), (2, 0))
    late_at = ((3, 1), (1, 1), (2, 1))
    total = add_terms(spans[0], early_at, lefts[0], *shared, early, None, "new")
    total = add_terms(spans[0], late_at, lefts[0], *shared, late, total, "add")
    for span, left in zip(spans[1:], lefts[1:]):
        total = add_terms(span, early_at + late_at, left, *shared, early + late, total, "rest")
    return total


def solution(mesh):
    fine = Mesh(mesh.devices.reshape(SIZES), (*GRP, *WIDE))
    return jax.shard_map(
        per_device,
        mesh=fine,
        in_specs=(
            P(GRP, WIDE, None, None),
            P(WIDE, GRP, None, None),
            P(GRP, WIDE, None, None),
            P(),
            P(),
            P(GRP, WIDE, None),
        ),
        out_specs=P(GRP, WIDE, None, None),
        check_vma=False,
    )
```

```python
import functools

import jax
import jax.numpy as jnp
from jax import lax
from jax.experimental import pallas as pl
from jax.experimental.pallas import tpu as pltpu
from jax.sharding import Mesh, PartitionSpec as P

GRP = ("x", "zl")
WIDE = ("y", "zh", "core")
SIZES = (4, 2, 4, 2, 2)
B = 128
ROWS = 8
COLS = 8
TERMS = 4


def terms_kernel(layout, offsets, first, place, ls, rs, act, *refs):
    lefts, (psi, up, down, west, east) = refs[:4], refs[4:9]
    steps = len(offsets)
    rights, rest = [refs[9 + where] for where in layout], refs[9 + max(layout) + 1 :]
    if first:
        hout, lbuf, rbuf, grid, inner, psem, lsem, rsem = rest
    else:
        hin, hout, lbuf, rbuf, grid, inner, psem, lsem, rsem = rest
    n = pl.program_id(0)
    here = place[0]
    core, zh, y, zl, x = here & 1, (here >> 1) & 1, (here >> 2) & 3, (here >> 4) & 1, here >> 5

    def chunk(step):
        return (x + offsets[step][0]) & 3, (zl + offsets[step][1]) & 1

    def left_copies(step, slot):
        p, _ = chunk(step)
        where = (p - y) & 3
        mine, theirs = lefts[2 * offsets[step][1] : 2 * offsets[step][1] + 2]
        return (
            pltpu.make_async_copy(mine.at[where], lbuf.at[slot, core], lsem.at[slot, 0]),
            pltpu.make_async_copy(theirs.at[where], lbuf.at[slot, 1 - core], lsem.at[slot, 1]),
        )

    def right_copy(step, slot):
        source = rights[step]
        if len(source.shape) == 5:
            source = source.at[chunk(step)[0]]
        return pltpu.make_async_copy(source, rbuf.at[slot], rsem.at[slot])

    def fetch(step, slot):
        for copy in (*left_copies(step, slot), right_copy(step, slot)):
            copy.start()

    psi_copies = [
        pltpu.make_async_copy(psi, grid.at[pl.ds(1, ROWS), pl.ds(1, COLS)], psem.at[0]),
        pltpu.make_async_copy(up, grid.at[pl.ds(0, 1), pl.ds(1, COLS)], psem.at[1]),
        pltpu.make_async_copy(down, grid.at[pl.ds(ROWS + 1, 1), pl.ds(1, COLS)], psem.at[2]),
        pltpu.make_async_copy(west, grid.at[:, pl.ds(0, 1)], psem.at[3]),
        pltpu.make_async_copy(east, grid.at[:, pl.ds(COLS + 1, 1)], psem.at[4]),
    ]

    @pl.when(n == 0)
    def _():
        for copy in psi_copies:
            copy.start()
        fetch(0, 0)

    for step in range(1, steps):

        @pl.when(n == step - 1)
        def _():
            fetch(step, step % 2)

    @pl.when(n == 0)
    def _():
        hout[...] = jnp.zeros_like(hout) if first else hin[...]
        for copy in psi_copies:
            copy.wait()

    slot = lax.rem(n, 2)
    for copy in left_copies(0, slot):
        copy.wait()
    pltpu.make_async_copy(rbuf.at[1 - slot], rbuf.at[slot], rsem.at[slot]).wait()

    base = 0
    for step in range(steps):
        p, q = chunk(step)
        base = jnp.where(n == step, TERMS * (2 * p + q), base)

    def one_row(row, carry):
        for w in range(TERMS):
            picked = grid[row + 1 + ls[base + w], pl.ds(1 + rs[base + w], COLS)]
            joined = jnp.concatenate([picked[c] for c in range(COLS)], axis=1)
            part = jnp.dot(lbuf[slot, w // 2, row, w % 2], joined, preferred_element_type=jnp.float32)
            for c in range(COLS):
                on = act[row, c, base + w].astype(jnp.float32)
                inner[c, pl.ds(pl.multiple_of(row * B, B), B), w * B : (w + 1) * B] = (
                    part[:, c * B : (c + 1) * B] * on
                ).astype(jnp.bfloat16)
        return carry

    lax.fori_loop(0, ROWS, one_row, 0, unroll=True)

    for c in range(COLS):
        joined = jnp.concatenate([rbuf[slot, c, w] for w in range(TERMS)], axis=1)
        part = lax.dot_general(
            inner[c], joined, (((1,), (1,)), ((), ())), preferred_element_type=jnp.float32
        ).reshape(ROWS, B, B)

        hout[:, c] += part


def add_terms(offsets, layout, lefts, place, ls, rs, act, psis, rights, total):
    steps = len(offsets)
    first = total is None
    anywhere = pl.BlockSpec(memory_space=pl.ANY)
    whole = pl.BlockSpec((ROWS, COLS, B, B), lambda n, *_: (0, 0, 0, 0), pipeline_mode=pl.Buffered(1))
    operands = [*lefts, *psis, *rights]
    in_specs = [anywhere] * len(operands)
    if not first:
        operands.append(total)
        in_specs.append(whole)
    return pl.pallas_call(
        functools.partial(terms_kernel, layout, offsets, first),
        out_shape=jax.ShapeDtypeStruct((ROWS, COLS, B, B), jnp.float32),
        grid_spec=pltpu.PrefetchScalarGridSpec(
            num_scalar_prefetch=4,
            grid=(steps,),
            in_specs=in_specs,
            out_specs=whole,
            scratch_shapes=[
                pltpu.VMEM((2, 2, ROWS, 2, B, B), jnp.bfloat16),
                pltpu.VMEM((2, COLS, TERMS, B, B), jnp.bfloat16),
                pltpu.VMEM((ROWS + 2, COLS + 2, B, B), jnp.bfloat16),
                pltpu.VMEM((COLS, ROWS * B, TERMS * B), jnp.bfloat16),
                pltpu.SemaphoreType.DMA((5,)),
                pltpu.SemaphoreType.DMA((2, 2)),
                pltpu.SemaphoreType.DMA((2,)),
            ],
        ),
        input_output_aliases={} if first else {4 + len(operands) - 1: 0},
        compiler_params=pltpu.CompilerParams(
            vmem_limit_bytes=56 << 20, dimension_semantics=("arbitrary",)
        ),
        cost_estimate=pl.CostEstimate(flops=1, bytes_accessed=1, transcendentals=0),
    )(place, ls, rs, act, *operands)


def ring(value, axis, shift):
    return lax.ppermute(value, axis, [(i, (i + shift) % 4) for i in range(4)])


def swap(value, axis):
    return lax.ppermute(value, axis, [(0, 1), (1, 0)])


def edges(value, axes, dim):
    count = lax.axis_size(axes)
    length = value.shape[dim]
    up = [(i, i + 1) for i in range(count - 1)]
    down = [(j, i) for i, j in up]
    last = lax.slice_in_dim(value, length - 1, length, axis=dim)
    leading = lax.slice_in_dim(value, 0, 1, axis=dim)
    return lax.ppermute(last, axes, up), lax.ppermute(leading, axes, down)


def after(values, events):
    held = lax.optimization_barrier((tuple(values), tuple(events)))
    return held[0]


def to_ring(value, axis):
    count = lax.axis_size(axis)
    return lax.all_to_all(jnp.broadcast_to(value[None], (count, *value.shape)), axis, 0, 0)


def around(value):
    return ring(value, "y", -1), ring(value, "y", 2), ring(value, "y", 1)


def per_device(left_env, right_env, psi, left_shift, right_shift, active):
    place = lax.axis_index((*GRP, *WIDE)).astype(jnp.int32)[None]
    matched = lax.axis_index("zl") == lax.axis_index("zh")

    right_x = to_ring(right_env, "x")
    right_z = swap(right_env, "zl")
    left_z = swap(left_env, "zh")
    north, south = edges(psi, GRP, 0)

    left_z, north, south = after((left_z, north, south), ())
    near = jnp.where(matched, left_env, left_z)
    other = jnp.where(matched, left_z, left_env)
    near_ring = around(near)
    sides = jnp.concatenate([north[:, ::7], psi[:, ::7], south[:, ::7]], axis=0)
    west = lax.ppermute(sides[:, 1:], WIDE, [(i, i + 1) for i in range(15)])
    east = lax.ppermute(sides[:, :1], WIDE, [(i + 1, i) for i in range(15)])

    near_ring, other, right_z = after((near_ring, other, right_z), ())
    near_y = jnp.stack([near, *near_ring])
    near_yc = swap(near_y, "core")
    other_y = jnp.stack([other, *around(other)])
    other_yc = swap(other_y, "core")

    lefts = (near_y, near_yc, other_y, other_yc)
    shared = (place, left_shift, right_shift, active, (psi, north, south, west, east))
    total = add_terms(((0, 0),), (0,), (near_y, near_yc, near_y, near_yc), *shared, (right_env,), None)

    right_x, right_z = after((right_x, right_z), ())
    right_zm = ring(right_z, "x", 1)
    right_zp = ring(right_z, "x", -1)
    far = lax.dynamic_index_in_dim(right_x, (lax.axis_index("x") + 2) & 3, 0, keepdims=False)
    far_z = swap(far, "zl")
    total = add_terms(
        ((3, 0), (1, 0), (2, 0), (0, 1)), (0, 0, 0, 1), lefts, *shared, (right_x, right_z), total
    )
    return add_terms(
        ((3, 1), (1, 1), (2, 1)), (0, 1, 2), lefts, *shared, (right_zm, right_zp, far_z), total
    )


def solution(mesh):
    fine = Mesh(mesh.devices.reshape(SIZES), (*GRP, *WIDE))
    return jax.shard_map(
        per_device,
        mesh=fine,
        in_specs=(
            P(GRP, WIDE, None, None),
            P(WIDE, GRP, None, None),
            P(GRP, WIDE, None, None),
            P(),
            P(),
            P(GRP, WIDE, None),
        ),
        out_specs=P(GRP, WIDE, None, None),
        check_vma=False,
    )
```

```python
import functools

import jax
import jax.numpy as jnp
from jax import lax
from jax.experimental import pallas as pl
from jax.experimental.pallas import tpu as pltpu
from jax.sharding import Mesh, PartitionSpec as P

GRP = ("x", "zl")
WIDE = ("y", "zh", "core")
SIZES = (4, 2, 4, 2, 2)
B = 128
ROWS = 8
COLS = 8
TERMS = 4


def terms_kernel(layout, offsets, first, place, ls, rs, act, *refs):
    whole, whole_other, turned, turned_other, psi, up, down, west, east = refs[:9]
    rights, rest = [], refs[9:]
    for pieces in layout:
        rights.append(rest[:pieces])
        rest = rest[pieces:]
    hin = None
    if not first:
        hin, rest = rest[0], rest[1:]
    hout, lbuf, rbuf, grid, inner, acc, psem, lsem, rsem, hsem = rest
    steps = len(layout)
    n = pl.program_id(0)
    here = place[0]
    core, zh, y, zl, x = here & 1, (here >> 1) & 1, (here >> 2) & 3, (here >> 4) & 1, here >> 5

    def chunk(step):
        return (x + offsets[step][0]) & 3, (zl + offsets[step][1]) & 1

    def left_copies(step, slot, own):
        p, _ = chunk(step)
        mine, theirs, where = (whole, whole_other, p) if own else (turned, turned_other, (p - y) & 3)
        return (
            pltpu.make_async_copy(mine.at[where], lbuf.at[slot, core], lsem.at[slot, 0]),
            pltpu.make_async_copy(theirs.at[where], lbuf.at[slot, 1 - core], lsem.at[slot, 1]),
        )

    def right_copies(step, slot):
        pieces = rights[step]
        sources = pieces if len(pieces) == 2 else [pieces[0].at[pl.ds(4 * h, 4)] for h in range(2)]
        return [
            pltpu.make_async_copy(sources[h], rbuf.at[slot, pl.ds(4 * h, 4)], rsem.at[slot, h])
            for h in range(2)
        ]

    def fetch(step, slot):
        for copy in right_copies(step, slot):
            copy.start()

        @pl.when(chunk(step)[1] == zh)
        def _():
            for copy in left_copies(step, slot, True):
                copy.start()

        @pl.when(chunk(step)[1] != zh)
        def _():
            for copy in left_copies(step, slot, False):
                copy.start()

    psi_copies = [
        pltpu.make_async_copy(psi, grid.at[pl.ds(1, ROWS), pl.ds(1, COLS)], psem.at[0]),
        pltpu.make_async_copy(up, grid.at[pl.ds(0, 1), pl.ds(1, COLS)], psem.at[1]),
        pltpu.make_async_copy(down, grid.at[pl.ds(ROWS + 1, 1), pl.ds(1, COLS)], psem.at[2]),
        pltpu.make_async_copy(west, grid.at[:, pl.ds(0, 1)], psem.at[3]),
        pltpu.make_async_copy(east, grid.at[:, pl.ds(COLS + 1, 1)], psem.at[4]),
    ]

    @pl.when(n == 0)
    def _():
        for copy in psi_copies:
            copy.start()
        fetch(0, 0)
        if not first:
            pltpu.make_async_copy(hin, acc, hsem.at[COLS]).start()

    for step in range(1, steps):

        @pl.when(n == step - 1)
        def _():
            fetch(step, step % 2)

    @pl.when(n == 0)
    def _():
        if first:
            acc[...] = jnp.zeros_like(acc)
        for copy in psi_copies:
            copy.wait()

    slot = lax.rem(n, 2)
    for copy in left_copies(0, slot, True):
        copy.wait()
    for copy in right_copies(0, slot):
        copy.wait()

    base = 0
    for step in range(steps):
        p, q = chunk(step)
        base = jnp.where(n == step, TERMS * (2 * p + q), base)

    def one_row(row, carry):
        for w in range(TERMS):
            picked = grid[row + 1 + ls[base + w], pl.ds(1 + rs[base + w], COLS)]
            joined = jnp.concatenate([picked[c] for c in range(COLS)], axis=1)
            part = jnp.dot(lbuf[slot, w // 2, row, w % 2], joined, preferred_element_type=jnp.float32)
            for c in range(COLS):
                on = act[row, c, base + w].astype(jnp.float32)
                inner[c, pl.ds(pl.multiple_of(row * B, B), B), w * B : (w + 1) * B] = (
                    part[:, c * B : (c + 1) * B] * on
                ).astype(jnp.bfloat16)
        return carry

    lax.fori_loop(0, ROWS, one_row, 0, unroll=True)

    if not first:

        @pl.when(n == 0)
        def _():
            pltpu.make_async_copy(hin, acc, hsem.at[COLS]).wait()

    outward = [pltpu.make_async_copy(acc.at[:, c], hout.at[:, c], hsem.at[c]) for c in range(COLS)]
    for half in range(2):
        columns = range(half * COLS // 2, (half + 1) * COLS // 2)
        for c in columns:
            joined = jnp.concatenate([rbuf[slot, c, w] for w in range(TERMS)], axis=1)
            part = lax.dot_general(
                inner[c], joined, (((1,), (1,)), ((), ())), preferred_element_type=jnp.float32
            ).reshape(ROWS, B, B)
            acc[:, c] += part

        @pl.when(n == steps - 1)
        def _():
            for c in columns:
                outward[c].start()

    @pl.when(n == steps - 1)
    def _():
        for copy in outward:
            copy.wait()


def add_terms(offsets, lefts, place, ls, rs, act, psis, rights, total):
    steps = len(rights)
    layout = tuple(len(pieces) for pieces in rights)
    first = total is None
    anywhere = pl.BlockSpec(memory_space=pl.ANY)
    operands = [*lefts, *psis, *(piece for pieces in rights for piece in pieces)]
    in_specs = [anywhere] * len(operands)
    if not first:
        operands.append(total)
        in_specs.append(anywhere)
    return pl.pallas_call(
        functools.partial(terms_kernel, layout, offsets, first),
        out_shape=jax.ShapeDtypeStruct((ROWS, COLS, B, B), jnp.float32),
        grid_spec=pltpu.PrefetchScalarGridSpec(
            num_scalar_prefetch=4,
            grid=(steps,),
            in_specs=in_specs,
            out_specs=anywhere,
            scratch_shapes=[
                pltpu.VMEM((2, 2, ROWS, 2, B, B), jnp.bfloat16),
                pltpu.VMEM((2, COLS, TERMS, B, B), jnp.bfloat16),
                pltpu.VMEM((ROWS + 2, COLS + 2, B, B), jnp.bfloat16),
                pltpu.VMEM((COLS, ROWS * B, TERMS * B), jnp.bfloat16),
                pltpu.VMEM((ROWS, COLS, B, B), jnp.float32),
                pltpu.SemaphoreType.DMA((5,)),
                pltpu.SemaphoreType.DMA((2, 2)),
                pltpu.SemaphoreType.DMA((2, 2)),
                pltpu.SemaphoreType.DMA((COLS + 1,)),
            ],
        ),
        input_output_aliases={} if first else {4 + len(operands) - 1: 0},
        compiler_params=pltpu.CompilerParams(
            vmem_limit_bytes=56 << 20, dimension_semantics=("arbitrary",)
        ),
        cost_estimate=pl.CostEstimate(flops=1, bytes_accessed=1, transcendentals=0),
    )(place, ls, rs, act, *operands)


def ring(value, axis, shift):
    return lax.ppermute(value, axis, [(i, (i + shift) % 4) for i in range(4)])


def swap(value, axis):
    return lax.ppermute(value, axis, [(0, 1), (1, 0)])


def edges(value, axes, dim):
    count = lax.axis_size(axes)
    length = value.shape[dim]
    up = [(i, i + 1) for i in range(count - 1)]
    down = [(j, i) for i, j in up]
    last = lax.slice_in_dim(value, length - 1, length, axis=dim)
    leading = lax.slice_in_dim(value, 0, 1, axis=dim)
    return lax.ppermute(last, axes, up), lax.ppermute(leading, axes, down)


def after(values, events):
    held = lax.optimization_barrier((tuple(values), tuple(events)))
    return held[0]


def per_device(left_env, right_env, psi, left_shift, right_shift, active):
    place = lax.axis_index((*GRP, *WIDE)).astype(jnp.int32)[None]

    left_y = lax.all_gather(left_env, "y", axis=0)
    left_z = swap(left_env, "zh")
    north, south = edges(psi, GRP, 0)

    north, south, own = after((north, south, right_env), ())
    right_m = ring(own, "x", 1)
    right_p = ring(own, "x", -1)

    left_z, own = after((left_z, own), ())
    right_z = swap(own, "zl")
    left_zm = ring(left_z, "y", 1)
    left_zp = ring(left_z, "y", -1)

    right_m, right_p, left_zm, left_zp, left_z = after((right_m, right_p, left_zm, left_zp, left_z), ())
    far_0 = ring(right_m[:4], "x", 1)
    far_1 = ring(right_p[4:], "x", -1)
    left_z2 = ring(left_z, "y", 2)
    sides = jnp.concatenate([north[:, ::7], psi[:, ::7], south[:, ::7]], axis=0)
    west = lax.ppermute(sides[:, 1:], WIDE, [(i, i + 1) for i in range(15)])
    east = lax.ppermute(sides[:, :1], WIDE, [(i + 1, i) for i in range(15)])

    right_z, far_0, far_1, left_z2, west, east = after(
        (right_z, far_0, far_1, left_z2, west, east), ()
    )
    right_zm = ring(right_z, "x", 1)
    right_zp = ring(right_z, "x", -1)
    far_z0 = swap(far_0, "zl")
    far_z1 = swap(far_1, "zl")
    left_yc = swap(left_y, "core")
    left_zs = jnp.stack([left_z, left_zp, left_z2, left_zm])
    left_zc = swap(left_zs, "core")

    shared = (
        (left_y, left_yc, left_zs, left_zc),
        place,
        left_shift,
        right_shift,
        active,
        (psi, north, south, west, east),
    )
    total = add_terms(
        ((0, 0), (0, 1), (3, 0), (1, 0), (2, 0)),
        *shared,
        [(right_env,), (right_z,), (right_m,), (right_p,), (far_0, far_1)],
        None,
    )
    return add_terms(
        ((3, 1), (1, 1), (2, 1)),
        *shared,
        [(right_zm,), (right_zp,), (far_z0, far_z1)],
        total,
    )


def solution(mesh):
    fine = Mesh(mesh.devices.reshape(SIZES), (*GRP, *WIDE))
    return jax.shard_map(
        per_device,
        mesh=fine,
        in_specs=(
            P(GRP, WIDE, None, None),
            P(WIDE, GRP, None, None),
            P(GRP, WIDE, None, None),
            P(),
            P(),
            P(GRP, WIDE, None),
        ),
        out_specs=P(GRP, WIDE, None, None),
        check_vma=False,
    )
```

```python
import functools

import jax
import jax.numpy as jnp
from jax import lax
from jax.experimental import pallas as pl
from jax.experimental.pallas import tpu as pltpu
from jax.sharding import Mesh, PartitionSpec as P

GRP = ("x", "zl")
WIDE = ("y", "zh", "core")
SIZES = (4, 2, 4, 2, 2)
B = 128
ROWS = 8
COLS = 8
TERMS = 4


def terms_kernel(layout, offsets, first, place, ls, rs, act, *refs):
    whole, whole_other, turned, turned_other, psi, up, down, west, east = refs[:9]
    rights, rest = [], refs[9:]
    for pieces in layout:
        rights.append(rest[:pieces])
        rest = rest[pieces:]
    hin = None
    if not first:
        hin, rest = rest[0], rest[1:]
    hout, lbuf, rbuf, grid, inner, acc, psem, lsem, rsem, hsem = rest
    steps = len(layout)
    n = pl.program_id(0)
    here = place[0]
    core, zh, y, zl, x = here & 1, (here >> 1) & 1, (here >> 2) & 3, (here >> 4) & 1, here >> 5

    def chunk(step):
        return (x + offsets[step][0]) & 3, (zl + offsets[step][1]) & 1

    def left_copies(step, slot, own):
        p, _ = chunk(step)
        mine, theirs, where = (whole, whole_other, p) if own else (turned, turned_other, (p - y) & 3)
        return (
            pltpu.make_async_copy(mine.at[where], lbuf.at[slot, core], lsem.at[slot, 0]),
            pltpu.make_async_copy(theirs.at[where], lbuf.at[slot, 1 - core], lsem.at[slot, 1]),
        )

    def right_copies(step, slot):
        pieces = rights[step]
        sources = pieces if len(pieces) == 2 else [pieces[0].at[pl.ds(4 * h, 4)] for h in range(2)]
        return [
            pltpu.make_async_copy(sources[h], rbuf.at[slot, pl.ds(4 * h, 4)], rsem.at[slot, h])
            for h in range(2)
        ]

    def fetch(step, slot):
        for copy in right_copies(step, slot):
            copy.start()

        @pl.when(chunk(step)[1] == zh)
        def _():
            for copy in left_copies(step, slot, True):
                copy.start()

        @pl.when(chunk(step)[1] != zh)
        def _():
            for copy in left_copies(step, slot, False):
                copy.start()

    psi_copies = [
        pltpu.make_async_copy(psi, grid.at[pl.ds(1, ROWS), pl.ds(1, COLS)], psem.at[0]),
        pltpu.make_async_copy(up, grid.at[pl.ds(0, 1), pl.ds(1, COLS)], psem.at[1]),
        pltpu.make_async_copy(down, grid.at[pl.ds(ROWS + 1, 1), pl.ds(1, COLS)], psem.at[2]),
        pltpu.make_async_copy(west, grid.at[:, pl.ds(0, 1)], psem.at[3]),
        pltpu.make_async_copy(east, grid.at[:, pl.ds(COLS + 1, 1)], psem.at[4]),
    ]

    @pl.when(n == 0)
    def _():
        for copy in psi_copies:
            copy.start()
        fetch(0, 0)
        if not first:
            pltpu.make_async_copy(hin, acc, hsem.at[COLS]).start()

    for step in range(1, steps):

        @pl.when(n == step - 1)
        def _():
            fetch(step, step % 2)

    @pl.when(n == 0)
    def _():
        if first:
            acc[...] = jnp.zeros_like(acc)
        for copy in psi_copies:
            copy.wait()

    slot = lax.rem(n, 2)
    for copy in left_copies(0, slot, True):
        copy.wait()
    for copy in right_copies(0, slot):
        copy.wait()

    base = 0
    for step in range(steps):
        p, q = chunk(step)
        base = jnp.where(n == step, TERMS * (2 * p + q), base)

    def one_row(row, carry):
        for w in range(TERMS):
            picked = grid[row + 1 + ls[base + w], pl.ds(1 + rs[base + w], COLS)]
            joined = jnp.concatenate([picked[c] for c in range(COLS)], axis=1)
            part = jnp.dot(lbuf[slot, w // 2, row, w % 2], joined, preferred_element_type=jnp.float32)
            for c in range(COLS):
                on = act[row, c, base + w].astype(jnp.float32)
                inner[c, pl.ds(pl.multiple_of(row * B, B), B), w * B : (w + 1) * B] = (
                    part[:, c * B : (c + 1) * B] * on
                ).astype(jnp.bfloat16)
        return carry

    lax.fori_loop(0, ROWS, one_row, 0, unroll=True)

    if not first:

        @pl.when(n == 0)
        def _():
            pltpu.make_async_copy(hin, acc, hsem.at[COLS]).wait()

    outward = [pltpu.make_async_copy(acc.at[:, c], hout.at[:, c], hsem.at[c]) for c in range(COLS)]
    for half in range(2):
        columns = range(half * COLS // 2, (half + 1) * COLS // 2)
        for c in columns:
            joined = jnp.concatenate([rbuf[slot, c, w] for w in range(TERMS)], axis=1)
            part = lax.dot_general(
                inner[c], joined, (((1,), (1,)), ((), ())), preferred_element_type=jnp.float32
            ).reshape(ROWS, B, B)
            acc[:, c] += part

        @pl.when(n == steps - 1)
        def _():
            for c in columns:
                outward[c].start()

    @pl.when(n == steps - 1)
    def _():
        for copy in outward:
            copy.wait()


def add_terms(offsets, lefts, place, ls, rs, act, psis, rights, total):
    steps = len(rights)
    layout = tuple(len(pieces) for pieces in rights)
    first = total is None
    anywhere = pl.BlockSpec(memory_space=pl.ANY)
    operands = [*lefts, *psis, *(piece for pieces in rights for piece in pieces)]
    in_specs = [anywhere] * len(operands)
    if not first:
        operands.append(total)
        in_specs.append(anywhere)
    return pl.pallas_call(
        functools.partial(terms_kernel, layout, offsets, first),
        out_shape=jax.ShapeDtypeStruct((ROWS, COLS, B, B), jnp.float32),
        grid_spec=pltpu.PrefetchScalarGridSpec(
            num_scalar_prefetch=4,
            grid=(steps,),
            in_specs=in_specs,
            out_specs=anywhere,
            scratch_shapes=[
                pltpu.VMEM((2, 2, ROWS, 2, B, B), jnp.bfloat16),
                pltpu.VMEM((2, COLS, TERMS, B, B), jnp.bfloat16),
                pltpu.VMEM((ROWS + 2, COLS + 2, B, B), jnp.bfloat16),
                pltpu.VMEM((COLS, ROWS * B, TERMS * B), jnp.bfloat16),
                pltpu.VMEM((ROWS, COLS, B, B), jnp.float32),
                pltpu.SemaphoreType.DMA((5,)),
                pltpu.SemaphoreType.DMA((2, 2)),
                pltpu.SemaphoreType.DMA((2, 2)),
                pltpu.SemaphoreType.DMA((COLS + 1,)),
            ],
        ),
        input_output_aliases={} if first else {4 + len(operands) - 1: 0},
        compiler_params=pltpu.CompilerParams(
            vmem_limit_bytes=56 << 20, dimension_semantics=("arbitrary",)
        ),
        cost_estimate=pl.CostEstimate(flops=1, bytes_accessed=1, transcendentals=0),
    )(place, ls, rs, act, *operands)


def ring(value, axis, shift):
    return lax.ppermute(value, axis, [(i, (i + shift) % 4) for i in range(4)])


def swap(value, axis):
    return lax.ppermute(value, axis, [(0, 1), (1, 0)])


def edges(value, axes, dim):
    count = lax.axis_size(axes)
    length = value.shape[dim]
    up = [(i, i + 1) for i in range(count - 1)]
    down = [(j, i) for i, j in up]
    last = lax.slice_in_dim(value, length - 1, length, axis=dim)
    leading = lax.slice_in_dim(value, 0, 1, axis=dim)
    return lax.ppermute(last, axes, up), lax.ppermute(leading, axes, down)


def after(values, events):
    held = lax.optimization_barrier((tuple(values), tuple(events)))
    return held[0]


def per_device(left_env, right_env, psi, left_shift, right_shift, active):
    place = lax.axis_index((*GRP, *WIDE)).astype(jnp.int32)[None]

    left_y = lax.all_gather(left_env, "y", axis=0)
    left_z = swap(left_env, "zh")
    north, south = edges(psi, GRP, 0)

    north, south, own = after((north, south, right_env), ())
    right_m = ring(own, "x", 1)
    right_p = ring(own, "x", -1)

    left_z, own = after((left_z, own), ())
    right_z = swap(own, "zl")
    left_zm = ring(left_z, "y", 1)
    left_zp = ring(left_z, "y", -1)

    left_zm, left_zp, left_z = after((left_zm, left_zp, left_z), ())
    far_0 = ring(right_m[:4], "x", 1)
    far_1 = ring(right_p[4:], "x", -1)
    left_z2 = ring(left_z, "y", 2)
    sides = jnp.concatenate([north[:, ::7], psi[:, ::7], south[:, ::7]], axis=0)
    west = lax.ppermute(sides[:, 1:], WIDE, [(i, i + 1) for i in range(15)])
    east = lax.ppermute(sides[:, :1], WIDE, [(i + 1, i) for i in range(15)])

    right_z, far_0, far_1, left_z2, west, east = after(
        (right_z, far_0, far_1, left_z2, west, east), ()
    )
    right_zm = ring(right_z, "x", 1)
    right_zp = ring(right_z, "x", -1)
    far_z0 = swap(far_0, "zl")
    far_z1 = swap(far_1, "zl")
    left_yc = swap(left_y, "core")
    left_zs = jnp.stack([left_z, left_zp, left_z2, left_zm])
    left_zc = swap(left_zs, "core")

    shared = (
        (left_y, left_yc, left_zs, left_zc),
        place,
        left_shift,
        right_shift,
        active,
        (psi, north, south, west, east),
    )
    total = add_terms(
        ((0, 0), (0, 1), (3, 0), (1, 0), (2, 0)),
        *shared,
        [(right_env,), (right_z,), (right_m,), (right_p,), (far_0, far_1)],
        None,
    )
    return add_terms(
        ((3, 1), (1, 1), (2, 1)),
        *shared,
        [(right_zm,), (right_zp,), (far_z0, far_z1)],
        total,
    )


def solution(mesh):
    fine = Mesh(mesh.devices.reshape(SIZES), (*GRP, *WIDE))
    return jax.shard_map(
        per_device,
        mesh=fine,
        in_specs=(
            P(GRP, WIDE, None, None),
            P(WIDE, GRP, None, None),
            P(GRP, WIDE, None, None),
            P(),
            P(),
            P(GRP, WIDE, None),
        ),
        out_specs=P(GRP, WIDE, None, None),
        check_vma=False,
    )
```

```python
import functools

import jax
import jax.numpy as jnp
from jax import lax
from jax.experimental import pallas as pl
from jax.experimental.pallas import tpu as pltpu
from jax.sharding import Mesh, PartitionSpec as P

GRP = ("x", "zl")
WIDE = ("y", "zh", "core")
SIZES = (4, 2, 4, 2, 2)
B = 128
ROWS = 8
COLS = 8
TERMS = 4


def terms_kernel(layout, offsets, first, place, ls, rs, act, *refs):
    whole, whole_other, turned, turned_other, psi, up, down, west, east = refs[:9]
    rights, rest = [], refs[9:]
    for pieces in layout:
        rights.append(rest[:pieces])
        rest = rest[pieces:]
    hin = None
    if not first:
        hin, rest = rest[0], rest[1:]
    hout, lbuf, rbuf, grid, inner, acc, psem, lsem, rsem, hsem = rest
    steps = len(layout)
    n = pl.program_id(0)
    here = place[0]
    core, zh, y, zl, x = here & 1, (here >> 1) & 1, (here >> 2) & 3, (here >> 4) & 1, here >> 5

    def chunk(step):
        return (x + offsets[step][0]) & 3, (zl + offsets[step][1]) & 1

    def left_copies(step, slot, own):
        p, _ = chunk(step)
        mine, theirs, where = (whole, whole_other, p) if own else (turned, turned_other, (p - y) & 3)
        return (
            pltpu.make_async_copy(mine.at[where], lbuf.at[slot, core], lsem.at[slot, 0]),
            pltpu.make_async_copy(theirs.at[where], lbuf.at[slot, 1 - core], lsem.at[slot, 1]),
        )

    def right_copies(step, slot):
        pieces = rights[step]
        sources = pieces if len(pieces) == 2 else [pieces[0].at[pl.ds(4 * h, 4)] for h in range(2)]
        return [
            pltpu.make_async_copy(sources[h], rbuf.at[slot, pl.ds(4 * h, 4)], rsem.at[slot, h])
            for h in range(2)
        ]

    def fetch(step, slot):
        for copy in right_copies(step, slot):
            copy.start()

        @pl.when(chunk(step)[1] == zh)
        def _():
            for copy in left_copies(step, slot, True):
                copy.start()

        @pl.when(chunk(step)[1] != zh)
        def _():
            for copy in left_copies(step, slot, False):
                copy.start()

    psi_copies = [
        pltpu.make_async_copy(psi, grid.at[pl.ds(1, ROWS), pl.ds(1, COLS)], psem.at[0]),
        pltpu.make_async_copy(up, grid.at[pl.ds(0, 1), pl.ds(1, COLS)], psem.at[1]),
        pltpu.make_async_copy(down, grid.at[pl.ds(ROWS + 1, 1), pl.ds(1, COLS)], psem.at[2]),
        pltpu.make_async_copy(west, grid.at[:, pl.ds(0, 1)], psem.at[3]),
        pltpu.make_async_copy(east, grid.at[:, pl.ds(COLS + 1, 1)], psem.at[4]),
    ]

    @pl.when(n == 0)
    def _():
        for copy in psi_copies:
            copy.start()
        fetch(0, 0)
        if not first:
            pltpu.make_async_copy(hin, acc, hsem.at[COLS]).start()

    for step in range(1, steps):

        @pl.when(n == step - 1)
        def _():
            fetch(step, step % 2)

    @pl.when(n == 0)
    def _():
        if first:
            acc[...] = jnp.zeros_like(acc)
        for copy in psi_copies:
            copy.wait()

    slot = lax.rem(n, 2)
    for copy in left_copies(0, slot, True):
        copy.wait()
    for copy in right_copies(0, slot):
        copy.wait()

    base = 0
    for step in range(steps):
        p, q = chunk(step)
        base = jnp.where(n == step, TERMS * (2 * p + q), base)

    def one_row(row, carry):
        for w in range(TERMS):
            picked = grid[row + 1 + ls[base + w], pl.ds(1 + rs[base + w], COLS)]
            joined = jnp.concatenate([picked[c] for c in range(COLS)], axis=1)
            part = jnp.dot(lbuf[slot, w // 2, row, w % 2], joined, preferred_element_type=jnp.float32)
            for c in range(COLS):
                on = act[row, c, base + w].astype(jnp.float32)
                inner[c, pl.ds(pl.multiple_of(row * B, B), B), w * B : (w + 1) * B] = (
                    part[:, c * B : (c + 1) * B] * on
                ).astype(jnp.bfloat16)
        return carry

    lax.fori_loop(0, ROWS, one_row, 0, unroll=True)

    if not first:

        @pl.when(n == 0)
        def _():
            pltpu.make_async_copy(hin, acc, hsem.at[COLS]).wait()

    outward = [pltpu.make_async_copy(acc.at[:, c], hout.at[:, c], hsem.at[c]) for c in range(COLS)]
    for half in range(2):
        columns = range(half * COLS // 2, (half + 1) * COLS // 2)
        for c in columns:
            joined = jnp.concatenate([rbuf[slot, c, w] for w in range(TERMS)], axis=1)
            part = lax.dot_general(
                inner[c], joined, (((1,), (1,)), ((), ())), preferred_element_type=jnp.float32
            ).reshape(ROWS, B, B)
            acc[:, c] += part

        @pl.when(n == steps - 1)
        def _():
            for c in columns:
                outward[c].start()

    @pl.when(n == steps - 1)
    def _():
        for copy in outward:
            copy.wait()


def add_terms(offsets, lefts, place, ls, rs, act, psis, rights, total):
    steps = len(rights)
    layout = tuple(len(pieces) for pieces in rights)
    first = total is None
    anywhere = pl.BlockSpec(memory_space=pl.ANY)
    operands = [*lefts, *psis, *(piece for pieces in rights for piece in pieces)]
    in_specs = [anywhere] * len(operands)
    if not first:
        operands.append(total)
        in_specs.append(anywhere)
    return pl.pallas_call(
        functools.partial(terms_kernel, layout, offsets, first),
        out_shape=jax.ShapeDtypeStruct((ROWS, COLS, B, B), jnp.float32),
        grid_spec=pltpu.PrefetchScalarGridSpec(
            num_scalar_prefetch=4,
            grid=(steps,),
            in_specs=in_specs,
            out_specs=anywhere,
            scratch_shapes=[
                pltpu.VMEM((2, 2, ROWS, 2, B, B), jnp.bfloat16),
                pltpu.VMEM((2, COLS, TERMS, B, B), jnp.bfloat16),
                pltpu.VMEM((ROWS + 2, COLS + 2, B, B), jnp.bfloat16),
                pltpu.VMEM((COLS, ROWS * B, TERMS * B), jnp.bfloat16),
                pltpu.VMEM((ROWS, COLS, B, B), jnp.float32),
                pltpu.SemaphoreType.DMA((5,)),
                pltpu.SemaphoreType.DMA((2, 2)),
                pltpu.SemaphoreType.DMA((2, 2)),
                pltpu.SemaphoreType.DMA((COLS + 1,)),
            ],
        ),
        input_output_aliases={} if first else {4 + len(operands) - 1: 0},
        compiler_params=pltpu.CompilerParams(
            vmem_limit_bytes=32 << 20, dimension_semantics=("arbitrary",)
        ),
        cost_estimate=pl.CostEstimate(flops=1, bytes_accessed=1, transcendentals=0),
    )(place, ls, rs, act, *operands)


def ring(value, axis, shift):
    return lax.ppermute(value, axis, [(i, (i + shift) % 4) for i in range(4)])


def swap(value, axis):
    return lax.ppermute(value, axis, [(0, 1), (1, 0)])


def edges(value, axes, dim):
    count = lax.axis_size(axes)
    length = value.shape[dim]
    up = [(i, i + 1) for i in range(count - 1)]
    down = [(j, i) for i, j in up]
    last = lax.slice_in_dim(value, length - 1, length, axis=dim)
    leading = lax.slice_in_dim(value, 0, 1, axis=dim)
    return lax.ppermute(last, axes, up), lax.ppermute(leading, axes, down)


def after(values, events):
    held = lax.optimization_barrier((tuple(values), tuple(events)))
    return held[0]


def per_device(left_env, right_env, psi, left_shift, right_shift, active):
    place = lax.axis_index((*GRP, *WIDE)).astype(jnp.int32)[None]

    left_y = lax.all_gather(left_env, "y", axis=0)
    left_z = swap(left_env, "zh")
    north, south = edges(psi, GRP, 0)

    north, south, own = after((north, south, right_env), ())
    right_m = ring(own, "x", 1)
    right_p = ring(own, "x", -1)

    left_z, own = after((left_z, own), ())
    right_z = swap(own, "zl")
    left_zm = ring(left_z, "y", 1)
    left_zp = ring(left_z, "y", -1)

    left_zm, left_zp, left_z = after((left_zm, left_zp, left_z), ())
    far_0 = ring(right_m[:4], "x", 1)
    far_1 = ring(right_p[4:], "x", -1)
    left_z2 = ring(left_z, "y", 2)
    sides = jnp.concatenate([north[:, ::7], psi[:, ::7], south[:, ::7]], axis=0)
    west = lax.ppermute(sides[:, 1:], WIDE, [(i, i + 1) for i in range(15)])
    east = lax.ppermute(sides[:, :1], WIDE, [(i + 1, i) for i in range(15)])

    right_z, far_0, far_1, left_z2, west, east = after(
        (right_z, far_0, far_1, left_z2, west, east), ()
    )
    right_zm = ring(right_z, "x", 1)
    right_zp = ring(right_z, "x", -1)
    far_z0 = swap(far_0, "zl")
    far_z1 = swap(far_1, "zl")
    left_yc = swap(left_y, "core")
    left_zs = jnp.stack([left_z, left_zp, left_z2, left_zm])
    left_zc = swap(left_zs, "core")

    shared = (
        (left_y, left_yc, left_zs, left_zc),
        place,
        left_shift,
        right_shift,
        active,
        (psi, north, south, west, east),
    )
    total = add_terms(
        ((0, 0), (0, 1), (3, 0), (1, 0), (2, 0)),
        *shared,
        [(right_env,), (right_z,), (right_m,), (right_p,), (far_0, far_1)],
        None,
    )
    return add_terms(
        ((3, 1), (1, 1), (2, 1)),
        *shared,
        [(right_zm,), (right_zp,), (far_z0, far_z1)],
        total,
    )


def solution(mesh):
    fine = Mesh(mesh.devices.reshape(SIZES), (*GRP, *WIDE))
    return jax.shard_map(
        per_device,
        mesh=fine,
        in_specs=(
            P(GRP, WIDE, None, None),
            P(WIDE, GRP, None, None),
            P(GRP, WIDE, None, None),
            P(),
            P(),
            P(GRP, WIDE, None),
        ),
        out_specs=P(GRP, WIDE, None, None),
        check_vma=False,
    )
```
